32 devices in a mesh: ctx: 8 (over y, x, core), head: 4 (over z).
Axes of the slice: x: 2, y: 2, z: 4, core: 2. Of those that a mesh axis runs over, the one named last changes fastest.
Arguments:
- query_rows: bfloat16 [16384, 8192], P('ctx', 'head'), may hold values from -0.3984375 to 0.3984375
- key_rows: bfloat16 [16384, 8192], P('ctx', 'head'), may hold values from -6 to 6
- value_rows: bfloat16 [16384, 8192], P('ctx', 'head'), may hold values from -6 to 6
- level_weights: float32 [17, 32, 16384], P(None, 'head', 'ctx'), may hold values from 0.2 to 2
Outputs:
- attended: bfloat16 [16384, 8192], P(('ctx', 'head'))
The draws below stay inside these ranges and needn't reach their ends.
All inputs are finite; a program needn't handle non-finite values.
Results may differ from the reference program's by a relative error of at most 0.0049.
Values may be sent and summed in bfloat16 or wider, within the bound.
No kernel may reach another device: no remote copies, remote signals or barrier semaphores. Data moves between devices by JAX's collectives and lax.ppermute only.
A program may use at most 192 MiB of HBM per device.

```python
import math
import jax
import jax.numpy as jnp
from jax import lax

HEADS = 32
HDIM = 256
BLK = 512
LEVELS = 17
WIDTH = 8192
TOKENS = 16384


def shard_levels(rng, dims, pieces, smallest, largest):
    loudness = 1.0
    for position, shards_of in pieces:
        draws = jax.random.uniform(jax.random.fold_in(jax.random.fold_in(rng, 6), position), (shards_of,), jnp.float32, smallest / len(pieces), largest / len(pieces))
        loudness = loudness * jnp.repeat(jnp.exp(draws), dims[position] // shards_of).reshape((-1,) + (1,) * (len(dims) - 1 - position))
    return loudness


def noise(rng, extent, deviation, limit, split=(), dtype=jnp.bfloat16):
    values = jax.random.normal(rng, extent, jnp.float32) * deviation
    if len(split) > 0:
        values = shard_levels(rng, extent, split, -0.22, 0.18) * values
    return jnp.clip(values, min=-limit, max=limit).astype(dtype)


def setup_inputs(seed: int = 0) -> dict:
    splits = jax.random.split(jax.random.key(seed), 5)
    return {
        "query_rows": noise(splits[0], (TOKENS, WIDTH), 0.0625, 0.3984375, ((0, 8), (1, 4))),
        "key_rows": noise(splits[1], (TOKENS, WIDTH), 1.0, 6.0, ((0, 8), (1, 4))),
        "value_rows": noise(splits[2], (TOKENS, WIDTH), 1.0, 6.0, ((0, 8), (1, 4))),
        "level_weights": jnp.clip(jnp.exp(math.log(2.0) - 2.3025851 * jax.random.uniform(splits[3], (LEVELS, HEADS, TOKENS), jnp.float32) ** shard_levels(splits[3], (LEVELS, HEADS, TOKENS), ((1, 4), (2, 8)), -0.2, 0.2)), 0.2, 2.0),
    }


def level_grid(size):
    rows_index = lax.broadcasted_iota(jnp.int32, (size, size), 0)
    cols_index = lax.broadcasted_iota(jnp.int32, (size, size), 1)
    xored = jnp.bitwise_xor(rows_index, cols_index)
    grid = jnp.zeros((size, size), jnp.int32)
    for power in range(size.bit_length() - 1):
        grid = grid + (xored >= 2 ** power).astype(jnp.int32)
    return grid, cols_index <= rows_index


def level_scale():
    levels_index = jnp.arange(LEVELS).astype(jnp.float32)
    return jnp.exp2(-0.5 * jnp.maximum(levels_index - 1.0, 0.0))


def reference(query_rows, key_rows, value_rows, level_weights):
    blocks = TOKENS // BLK
    block_bits = BLK.bit_length() - 1
    global_bits = blocks.bit_length() - 1
    highest = lax.Precision.HIGHEST
    scaled = level_weights * level_scale()[:, None, None]
    per_head = scaled.reshape(LEVELS, HEADS, blocks, BLK).transpose(1, 0, 2, 3)

    def split_heads(rows_in):
        return rows_in.reshape(blocks, BLK, HEADS, HDIM).transpose(2, 0, 1, 3)

    grid, causal = level_grid(BLK)
    later_block = jnp.arange(blocks).astype(jnp.int32)[:, None]
    earlier_block = jnp.arange(blocks).astype(jnp.int32)[None, :]

    def one_head(inputs):
        queries_head, keys_head, values_head, weights_head = inputs
        query_float = queries_head.astype(jnp.float32)
        key_float = keys_head.astype(jnp.float32)
        value_float = values_head.astype(jnp.float32)
        scores = jnp.einsum("ntd,nsd->nts", query_float, key_float, precision=highest)
        weight_table = jnp.zeros((blocks, BLK, BLK), jnp.float32)
        for level in range(block_bits + 1):
            weight_table = weight_table + jnp.where(grid == level, weights_head[level][:, :, None], jnp.float32(0.0))
        weight_table = jnp.where(causal, weight_table, jnp.float32(0.0))
        weighted = (scores * weight_table).astype(jnp.bfloat16)
        output_sum = jnp.einsum("nts,nse->nte", weighted.astype(jnp.float32), value_float, precision=highest)
        states = jnp.einsum("ntd,nte->nde", key_float, value_float, precision=highest)
        for global_bit in range(global_bits):
            chosen = ((earlier_block < later_block) & (jnp.right_shift(jnp.bitwise_xor(later_block, earlier_block), global_bit) == 1)).astype(jnp.float32)
            level_state = jnp.einsum("nm,mde->nde", chosen, states, precision=highest).astype(jnp.bfloat16)
            product = jnp.einsum("ntd,nde->nte", query_float, level_state.astype(jnp.float32), precision=highest)
            output_sum = output_sum + product * weights_head[block_bits + 1 + global_bit][:, :, None]
        return output_sum

    result = lax.map(one_head, (split_heads(query_rows), split_heads(key_rows), split_heads(value_rows), per_head))
    return result.transpose(1, 2, 0, 3).reshape(TOKENS, HEADS * HDIM).astype(jnp.bfloat16)
```

```python
import functools

import jax
import jax.numpy as jnp
from jax import lax
from jax.experimental import pallas as pl
from jax.experimental.pallas import tpu as pltpu
from jax.sharding import PartitionSpec as P

BLK = 512
SUB = 128


def level_scale(levels):
    levels_index = jnp.arange(levels).astype(jnp.float32)
    return jnp.exp2(-0.5 * jnp.maximum(levels_index - 1.0, 0.0))


def exchange(rows, axis, bits):
    count = lax.axis_size(axis)
    return lax.ppermute(rows, axis, [(i, i ^ bits) for i in range(count)])


def local_slots(blocks):
    offsets, total, bit = [], 0, 0
    while (1 << bit) < blocks:
        offsets.append(total)
        total += blocks >> (bit + 1)
        bit += 1
    return offsets, max(total, 1)


def state_kernel(blocks, key_ref, value_ref, total_ref, level_ref):
    nodes = []
    for block in range(blocks):
        rows = pl.ds(block * BLK, BLK)
        nodes.append(
            lax.dot_general(
                key_ref[rows, :],
                value_ref[rows, :],
                (((0,), (0,)), ((), ())),
                preferred_element_type=jnp.float32,
            )
        )
    slot = 0
    while len(nodes) > 1:
        for left in nodes[::2]:
            level_ref[0, slot] = left.astype(jnp.bfloat16)
            slot += 1
        nodes = [nodes[i] + nodes[i + 1] for i in range(0, len(nodes), 2)]
    total_ref[0] = nodes[0]


def block_states(key_rows, value_rows, first, heads, size, blocks):
    slots = local_slots(blocks)[1]
    rows = blocks * BLK
    return pl.pallas_call(
        functools.partial(state_kernel, blocks),
        grid=(heads,),
        in_specs=[
            pl.BlockSpec((rows, size), lambda i: (0, first + i)),
            pl.BlockSpec((rows, size), lambda i: (0, first + i)),
        ],
        out_specs=[
            pl.BlockSpec((1, size, size), lambda i: (i, 0, 0)),
            pl.BlockSpec((1, slots, size, size), lambda i: (i, 0, 0, 0)),
        ],
        out_shape=[
            jax.ShapeDtypeStruct((heads, size, size), jnp.float32),
            jax.ShapeDtypeStruct((heads, slots, size, size), jnp.bfloat16),
        ],
        compiler_params=pltpu.CompilerParams(
            dimension_semantics=("arbitrary",), vmem_limit_bytes=40 << 20
        ),
        cost_estimate=pl.CostEstimate(
            flops=2 * heads * rows * size * size,
            bytes_accessed=4 * heads * rows * size,
            transcendentals=0,
        ),
        name="states",
    )(key_rows, value_rows)


def diagonal_weights(weights, rows):
    later = lax.broadcasted_iota(jnp.int32, (SUB, SUB), 0)
    earlier = lax.broadcasted_iota(jnp.int32, (SUB, SUB), 1)
    xored = jnp.bitwise_xor(later, earlier)
    table = jnp.broadcast_to(weights[rows : rows + SUB, 0:1], (SUB, SUB))
    for power in range(SUB.bit_length() - 1):
        column = weights[rows : rows + SUB, power + 1 : power + 2]
        table = jnp.where(xored >= 2**power, column, table)
    return jnp.where(earlier <= later, table, 0.0)


def local_block(query_ref, key_ref, value_ref, level_ref, weights, block, blocks):
    base = block * BLK
    half = 2 * SUB
    pieces = []
    for row in range(0, BLK, half):
        query = query_ref[pl.ds(base + row, half), :]
        keys = key_ref[pl.ds(base, row + half), :]
        scores = lax.dot_general(
            query, keys, (((1,), (1,)), ((), ())), preferred_element_type=jnp.float32
        )
        parts = []
        for t in range(row, row + half, SUB):
            line = []
            for s in range(0, row + half, SUB):
                tile = scores[t - row : t - row + SUB, s : s + SUB]
                if s < t:
                    level = (t ^ s).bit_length()
                    tile = tile * weights[t : t + SUB, level : level + 1]
                elif s == t:
                    tile = tile * diagonal_weights(weights, t)
                else:
                    tile = jnp.zeros_like(tile)
                line.append(tile.astype(jnp.bfloat16))
            parts.append(jnp.concatenate(line, axis=1))
        probs = jnp.concatenate(parts, axis=0)
        pieces.append(
            jnp.dot(
                probs,
                value_ref[pl.ds(base, row + half), :],
                preferred_element_type=jnp.float32,
            )
        )
    out = jnp.concatenate(pieces, axis=0)
    offsets = local_slots(blocks)[0]
    block_bits = BLK.bit_length() - 1
    query = query_ref[pl.ds(base, BLK), :]
    for bit, offset in enumerate(offsets):
        if (block >> bit) & 1:
            product = jnp.dot(
                query,
                level_ref[0, offset + (block >> (bit + 1))],
                preferred_element_type=jnp.float32,
            )
            level = block_bits + 1 + bit
            out = out + product * weights[:, level : level + 1]
    return out


def remote_block(query_ref, remote_ref, weights, block, first_level, bits):
    me = lax.axis_index("ctx")
    query = query_ref[pl.ds(block * BLK, BLK), :]
    total = None
    for bit in range(bits):
        product = jnp.dot(query, remote_ref[bit, 0], preferred_element_type=jnp.float32)
        here = ((me >> bit) & 1).astype(jnp.float32)
        level = first_level + bit
        term = product * (weights[:, level : level + 1] * here)
        total = term if total is None else total + term
    return total


def block_weights(weight_ref, block):
    return jnp.transpose(weight_ref[0, :, pl.ds(block * BLK, BLK)])


def split_out(outs, done, share):
    me = lax.axis_index("head")
    for place, out_ref in enumerate(outs):
        target = pl.multiple_of((me ^ place) * share, share)
        out_ref[...] = done[pl.ds(target, share), :]


def whole_kernel(
    blocks, share, first_level, bits, query_ref, key_ref, value_ref, weight_ref, level_ref, remote_ref, *rest
):
    outs, done = rest[:-1], rest[-1]
    for block in range(blocks):
        weights = block_weights(weight_ref, block)
        out = local_block(query_ref, key_ref, value_ref, level_ref, weights, block, blocks)
        out = out + remote_block(query_ref, remote_ref, weights, block, first_level, bits)
        done[pl.ds(block * BLK, BLK), :] = out.astype(jnp.bfloat16)
    split_out(outs, done, share)


def inner_kernel(blocks, query_ref, key_ref, value_ref, weight_ref, level_ref, out_ref):
    for block in range(blocks):
        weights = block_weights(weight_ref, block)
        out_ref[pl.ds(block * BLK, BLK), :] = local_block(
            query_ref, key_ref, value_ref, level_ref, weights, block, blocks
        )


def outer_kernel(blocks, share, first_level, bits, query_ref, inner_ref, weight_ref, remote_ref, *rest):
    outs, done = rest[:-1], rest[-1]
    for block in range(blocks):
        weights = block_weights(weight_ref, block)
        rows = pl.ds(block * BLK, BLK)
        out = inner_ref[rows, :] + remote_block(query_ref, remote_ref, weights, block, first_level, bits)
        done[rows, :] = out.astype(jnp.bfloat16)
    split_out(outs, done, share)


def place_kernel(count, first, width, across, send_own, *refs):
    pieces, out_ref, sems = refs[: count], refs[-2], refs[-1]
    me = lax.axis_index("head")
    copies = []
    for index, piece in enumerate(pieces):
        place = index if send_own else index + 1
        column = pl.multiple_of((me ^ place) * across + first, 128)
        copy = pltpu.make_async_copy(piece, out_ref.at[:, pl.ds(column, width)], sems.at[index])
        copy.start()
        copies.append(copy)
    for copy in copies:
        copy.wait()


def local(query_rows, key_rows, value_rows, level_weights):
    levels, heads, _ = level_weights.shape
    rows, across = query_rows.shape
    size = across // heads
    blocks = rows // BLK
    groups = lax.axis_size("head")
    share = rows // groups
    bits = lax.axis_size("ctx").bit_length() - 1
    offsets, slots = local_slots(blocks)
    first_level = BLK.bit_length() + len(offsets)
    padded = -(-levels // 8) * 8
    scaled = level_weights * level_scale(levels)[:, None, None]
    weights = jnp.pad(jnp.transpose(scaled, (1, 0, 2)), ((0, 0), (0, padded - levels), (0, 0)))

    sizes = [1, 1, 2]
    while sum(sizes) > heads - 1:
        sizes.pop()
    if heads - sum(sizes) > 1:
        sizes.append(heads - 1 - sum(sizes))
    sizes.append(heads - sum(sizes))
    firsts = [sum(sizes[:i]) for i in range(len(sizes))]

    def exchange_states(total):
        found = []
        for bit in range(bits):
            found.append(exchange(total.astype(jnp.bfloat16), "ctx", 1 << bit))
            total = total + found[-1].astype(jnp.float32)
        return jnp.stack(found)

    def column(first):
        return pl.BlockSpec((rows, size), lambda i: (0, first + i))

    out_type = jax.ShapeDtypeStruct

    def params(limit=48):
        return pltpu.CompilerParams(
            dimension_semantics=("arbitrary",), vmem_limit_bytes=limit << 20
        )

    def weight_spec(first):
        return pl.BlockSpec((1, padded, rows), lambda i: (first + i, 0, 0))

    level_spec = pl.BlockSpec((1, slots, size, size), lambda i: (i, 0, 0, 0))
    remote_spec = pl.BlockSpec((bits, 1, size, size), lambda i: (0, i, 0, 0))
    piece_spec = pl.BlockSpec((share, size), lambda i: (0, i))

    def cost(count, levels):
        return pl.CostEstimate(
            flops=2 * count * rows * size * levels * size,
            bytes_accessed=10 * count * rows * size,
            transcendentals=0,
        )

    chunks = []
    for index, (first, count) in enumerate(zip(firsts, sizes)):
        total, siblings = block_states(key_rows, value_rows, first, count, size, blocks)
        remote = exchange_states(total)
        pieces = [out_type((share, count * size), jnp.bfloat16)] * groups
        scratch = [pltpu.VMEM((rows, size), jnp.bfloat16)]
        if index == 0:
            inner = pl.pallas_call(
                functools.partial(inner_kernel, blocks),
                grid=(count,),
                in_specs=[column(first)] * 3 + [weight_spec(first), level_spec],
                out_specs=pl.BlockSpec((rows, size), lambda i: (0, i)),
                out_shape=out_type((rows, count * size), jnp.float32),
                compiler_params=params(),
                cost_estimate=cost(count, 4),
                name="inner",
            )(query_rows, key_rows, value_rows, weights, siblings)
            outs = pl.pallas_call(
                functools.partial(outer_kernel, blocks, share, first_level, bits),
                grid=(count,),
                in_specs=[column(first), pl.BlockSpec((rows, size), lambda i: (0, i)), weight_spec(first), remote_spec],
                out_specs=[piece_spec] * groups,
                out_shape=pieces,
                scratch_shapes=scratch,
                compiler_params=params(),
                cost_estimate=cost(count, bits),
                name="outer",
            )(query_rows, inner, weights, remote)
        else:
            outs = pl.pallas_call(
                functools.partial(whole_kernel, blocks, share, first_level, bits),
                grid=(count,),
                in_specs=[column(first)] * 3 + [weight_spec(first), level_spec, remote_spec],
                out_specs=[piece_spec] * groups,
                out_shape=pieces,
                scratch_shapes=scratch,
                compiler_params=params(),
                cost_estimate=cost(count, 4 + bits),
                name="whole",
            )(query_rows, key_rows, value_rows, weights, siblings, remote)
        chunks.append(outs)

    arrived = []
    for outs in chunks:
        moved = {}
        for place in sorted(range(1, groups), reverse=True):
            moved[place] = exchange(outs[place], "head", place)
        arrived.append([outs[0]] + [moved[place] for place in range(1, groups)])

    result = None
    for first, count, pieces in zip(firsts, sizes, arrived):
        operands = list(pieces)
        specs = [pl.BlockSpec(memory_space=pltpu.VMEM)] * groups
        aliases = {}
        if result is not None:
            operands.append(result)
            specs.append(pl.BlockSpec(memory_space=pl.ANY))
            aliases = {groups: 0}
        result = pl.pallas_call(
            functools.partial(place_kernel, groups, first * size, count * size, across, True),
            in_specs=specs,
            out_specs=pl.BlockSpec(memory_space=pl.ANY),
            out_shape=out_type((share, groups * across), jnp.bfloat16),
            scratch_shapes=[pltpu.SemaphoreType.DMA((groups,))],
            input_output_aliases=aliases,
            cost_estimate=pl.CostEstimate(
                flops=0, bytes_accessed=4 * groups * share * count * size, transcendentals=0
            ),
            name="place",
        )(*operands)
    return result


def solution(mesh):
    in_specs = (P("ctx", "head"), P("ctx", "head"), P("ctx", "head"), P(None, "head", "ctx"))
    out_specs = P(("ctx", "head"), None)
    return jax.shard_map(local, mesh=mesh, in_specs=in_specs, out_specs=out_specs, check_vma=False)
```
